32 devices in a mesh: energy: 8 (over z, y), space: 4 (over x, core).
Axes of the slice: x: 2, y: 2, z: 4, core: 2. Of those that a mesh axis runs over, the one named last changes fastest.
Arguments:
- lesser: bfloat16 [2, 512, 4, 65536], P(None, 'energy', 'space'), may hold values from -6 to 6
- greater: bfloat16 [2, 512, 4, 65536], P(None, 'energy', 'space'), may hold values from -6 to 6
- vdiag: bfloat16 [4, 256, 256], P('space'), may hold values from -0.375 to 0.375
- vlower: bfloat16 [4, 256, 256], P('space'), may hold values from -0.375 to 0.375
- occupancy: int32 [4, 8], P('space'), may hold values from 1 to 32, 128 in all within a row
- tile_order: int32 [4, 512], P('space'), may hold values from 0 to 511, each once within a row
Outputs:
- interaction_diag: bfloat16 [2, 512, 4, 256, 256], P(None, 'energy', 'space')
- interaction_lower: bfloat16 [2, 512, 4, 256, 256], P(None, 'energy', 'space')
The draws below stay inside these ranges and needn't reach their ends.
Inputs may be any that keep to these rules, and one draw needn't show every extreme that they name: `occupancy`: for each block, the entries sum to 128 and the largest is exactly 32. `tile_order`: each row is a permutation of the tile numbers.
All inputs are finite; a program needn't handle non-finite values.
Results may differ from the reference program's by a relative error of at most 0.015.
Values may be sent and summed in bfloat16 or wider, within the bound.
A program may use at most 448 MiB of HBM per device.

```python
import math
import jax
import jax.numpy as jnp
import numpy as np
from jax import lax

B = 256
NE = 512
TILE = 128
NNZ = 128
NBLK = 4
NTILES = 512
MAXT = 32
N_ENERGY = 8


def shard_levels(key, extent, cuts, low, high):
    def one(axis_at, shards_of):
        draws = jax.random.uniform(jax.random.fold_in(jax.random.fold_in(key, 6), axis_at), (shards_of,), jnp.float32, low / len(cuts), high / len(cuts))
        return jnp.repeat(jnp.exp(draws), extent[axis_at] // shards_of).reshape((-1,) + (1,) * (len(extent) - axis_at - 1))

    level = one(*cuts[0])
    for cut in cuts[1:]:
        level = level * one(*cut)
    return level


def length_profile(count, total, most, slope):
    loads = [(1 << 20) // math.isqrt(grade ** slope) + 1 for grade in range(2, count + 1)]
    spare, given = total - most - (count - 1), [1] * (count - 1)
    while spare > 0:
        free = [i for i in range(count - 1) if given[i] < most]
        mass, left = sum([loads[i] for i in free]), spare
        for i in free:
            more = min(most - given[i], max(1, left * loads[i] // mass), spare)
            given[i] = given[i] + more
            spare = spare - more
    return np.array([most] + given)


def ragged(rng, count, total, limit, lean):
    if count == 2:
        one = jax.random.randint(rng, (), max(1, total - limit), min(limit, total - 1) + 1)
        return jnp.stack([one, total - one])
    tallies = jnp.asarray(length_profile(count, total, limit, lean), jnp.int32)
    pairs = (count - 1) // 2
    source_of, taker = tallies[1:1 + 2 * pairs:2], tallies[2:2 + 2 * pairs:2]
    room = jnp.minimum(source_of - 1, limit - taker)
    shifted = jax.random.randint(jax.random.fold_in(rng, 1), (pairs,), 0, 1 << 20) % (room + 1)
    tallies = tallies.at[1:1 + 2 * pairs:2].set(source_of - shifted).at[2:2 + 2 * pairs:2].set(taker + shifted)
    return tallies[jax.random.permutation(jax.random.fold_in(rng, 2), count)]


def centred(own_key, extent, scale, most, cuts=(), kind=jnp.bfloat16):
    level = shard_levels(own_key, extent, cuts, -0.22, 0.18) if cuts else 1.0
    values = jax.random.normal(own_key, extent, jnp.float32) * scale * level
    return jnp.minimum(jnp.maximum(values, -most), most).astype(kind)


def setup_inputs(seed: int = 0) -> dict:
    streams_of = jax.random.split(jax.random.key(seed), 7)
    lesser = centred(streams_of[0], (2, NE, NBLK, B * B), 1.0, 6.0, ((1, 8), (2, 4)))
    greater = centred(streams_of[1], (2, NE, NBLK, B * B), 1.0, 6.0, ((1, 8), (2, 4)))
    vdiag = centred(streams_of[2], (NBLK, B, B), B ** -0.5, 0.375, ((0, 4),))
    vlower = centred(streams_of[3], (NBLK, B, B), B ** -0.5, 0.375, ((0, 4),))
    occupancy = jax.vmap(lambda own: ragged(own, N_ENERGY, NNZ, MAXT, 2))(jax.random.split(streams_of[4], NBLK)).reshape((NBLK, N_ENERGY)).astype(jnp.int32)
    tile_order = jax.vmap(lambda own: jax.random.permutation(own, NTILES))(jax.random.split(streams_of[5], NBLK)).reshape((NBLK, NTILES)).astype(jnp.int32)
    return {"lesser": lesser, "greater": greater, "vdiag": vdiag, "vlower": vlower, "occupancy": occupancy, "tile_order": tile_order}


def listed_mask(counts, order):
    slot_ids = jnp.arange(MAXT, dtype=jnp.int32)
    flat_slot = jnp.arange(N_ENERGY, dtype=jnp.int32)[:, None] * MAXT + slot_ids[None, :]
    listing = jnp.where(slot_ids[None, :] < counts[:, None], order[flat_slot], NTILES)
    marks = jnp.zeros((NTILES + 1,), jnp.float32).at[listing.reshape(-1)].set(1.0)
    return jnp.repeat(marks[:NTILES], TILE)


def polar_block(lesser, greater, counts, order, block):
    first = lax.complex(lesser[0, :, block].astype(jnp.float32), lesser[1, :, block].astype(jnp.float32))
    second = lax.complex(greater[0, :, block].astype(jnp.float32), greater[1, :, block].astype(jnp.float32))
    spectrum = jnp.fft.fft(first, axis=0) * jnp.fft.ifft(second, axis=0)
    result = jnp.fft.ifft(spectrum, axis=0) * (NE ** 0.5)
    mask = listed_mask(counts[block], order[block])
    real_part = (jnp.real(result) * mask[None, :]).astype(jnp.bfloat16)
    imag_part = (jnp.imag(result) * mask[None, :]).astype(jnp.bfloat16)
    return jnp.stack([real_part, imag_part]).reshape(2, NE, B, B)


def left_mul(matrix, blocks):
    return jnp.einsum("ab,xebc->xeac", matrix.astype(jnp.float32), blocks.astype(jnp.float32))


def right_mul(blocks, matrix):
    return jnp.einsum("xeab,bc->xeac", blocks.astype(jnp.float32), matrix.astype(jnp.float32))


def reference(lesser, greater, vdiag, vlower, occupancy, tile_order):
    polars = [polar_block(lesser, greater, occupancy, tile_order, block) for block in range(NBLK)]
    diag_list = []
    lower_list = []
    for block in range(NBLK):
        middle = left_mul(vdiag[block], polars[block]).astype(jnp.bfloat16)
        diag_sum = right_mul(middle, vdiag[block])
        lower_sum = right_mul(middle, vlower[block].T)
        if block > 0:
            left = left_mul(vlower[block], polars[block - 1]).astype(jnp.bfloat16)
            diag_sum = diag_sum + right_mul(left, vlower[block].T)
            lower_sum = lower_sum + right_mul(left, vdiag[block - 1])
        if block + 1 < NBLK:
            right = left_mul(vlower[block + 1].T, polars[block + 1]).astype(jnp.bfloat16)
            diag_sum = diag_sum + right_mul(right, vlower[block + 1])
        diag_list.append(diag_sum.astype(jnp.bfloat16))
        lower_list.append(lower_sum.astype(jnp.bfloat16))
    return jnp.stack(diag_list, axis=2), jnp.stack(lower_list, axis=2)
```

```python
import functools

import jax
import jax.numpy as jnp
import numpy as np
from jax import lax
from jax.experimental import pallas as pl
from jax.experimental.pallas import tpu as pltpu
from jax.sharding import PartitionSpec as P

TILE = 128
NNZ = 128
BF16 = jnp.bfloat16
F32 = jnp.float32


def passed_along(value, axis, steps):
    count = lax.axis_size(axis)
    leading, last = (max(0, -steps), min(count, count - steps))
    return lax.ppermute(value, axis, [(source, source + steps) for source in range(leading, last)])


def fourier_table(energies):
    grid = np.arange(energies)
    phase = 2.0 * np.pi * ((grid[:, None] * grid[None, :]) % energies) / energies
    cos, sin = np.cos(phase), np.sin(phase)
    return jnp.asarray(np.block([[cos, sin], [-sin, cos]]), BF16)


def pack_body(ranks, most, per_rank, first, slots, counts, order, lesser, greater, packed, listing, stage, sem, out_sem):
    def rank_step(r, j):
        def slot_step(s, j):
            tile = order[r * most + s]
            listing[j] = tile
            slot = j % per_rank - first

            @pl.when((slot >= 0) & (slot < slots))
            def _():
                columns = pl.ds(pl.multiple_of(tile * TILE, TILE), TILE)
                for which, source in enumerate((lesser, greater)):
                    pltpu.make_async_copy(
                        source.at[:, :, columns], stage.at[j // per_rank, slot, which], sem
                    ).start()

            return j + 1

        return lax.fori_loop(0, counts[r], slot_step, j)

    lax.fori_loop(0, ranks, rank_step, 0)
    pltpu.make_async_copy(stage, stage, sem).wait()
    written = pltpu.make_async_copy(stage, packed, out_sem)
    written.start()
    written.wait()


def pack(counts, order, lesser, greater, ranks, per_rank, first, slots):
    local = lesser.shape[1]
    anywhere = pl.BlockSpec(memory_space=pl.ANY)
    scalars = pl.BlockSpec(memory_space=pltpu.SMEM)
    moved = 2 * ranks * slots * 4 * local * TILE * 2
    return pl.pallas_call(
        functools.partial(pack_body, ranks, 2 * NNZ // ranks, per_rank, first, slots),
        out_shape=(
            jax.ShapeDtypeStruct((ranks, slots, 2, 2, local, TILE), BF16),
            jax.ShapeDtypeStruct((NNZ,), jnp.int32),
        ),
        in_specs=[scalars, scalars, anywhere, anywhere],
        out_specs=(anywhere, scalars),
        scratch_shapes=[
            pltpu.VMEM((ranks, slots, 2, 2, local, TILE), BF16),
            pltpu.SemaphoreType.DMA,
            pltpu.SemaphoreType.DMA,
        ],
        compiler_params=pltpu.CompilerParams(vmem_limit_bytes=16 << 20),
        cost_estimate=pl.CostEstimate(flops=0, bytes_accessed=moved, transcendentals=0),
        name="pack",
    )(counts, order, lesser, greater)


def correlate_body(tiles, halves, factor, table, data, *rest):
    outs = rest[-halves:]
    ranks, _, _, _, local, _ = data.shape
    energies = ranks * local

    def part(tile, which, p):
        value = data[:, tile, which, p]
        if local % 16:
            return value.astype(F32).reshape(energies, TILE).astype(BF16)
        return value.reshape(energies, TILE)

    def columns(which, order):
        return jnp.concatenate(
            [jnp.concatenate([part(t, which, p) for p in order], axis=0) for t in range(tiles)],
            axis=1,
        )

    first = jnp.dot(table[...], columns(0, (0, 1)), preferred_element_type=F32)
    second = jnp.dot(table[...], columns(1, (1, 0)), preferred_element_type=F32)
    first_re, first_im = first[:energies], first[energies:]
    second_im, second_re = second[:energies], second[energies:]
    product = jnp.concatenate(
        [
            (first_re * second_im + first_im * second_re).astype(BF16),
            (first_re * second_re - first_im * second_im).astype(BF16),
        ],
        axis=0,
    )
    polar = jnp.dot(table[...], product, preferred_element_type=F32) * factor
    step = local // halves
    for t in range(tiles):
        for p in range(2):
            value = polar[(1 - p) * energies:(2 - p) * energies, t * TILE:(t + 1) * TILE]
            value = value.reshape(ranks, local, TILE).astype(BF16)
            for h in range(halves):
                outs[h][:, t, p] = value[:, h * step:(h + 1) * step]


def correlate(table, data, per_rank, first, halves, previous):
    ranks, slots, _, _, local, _ = data.shape
    energies = ranks * local
    tiles = 2 if slots % 2 == 0 else 1
    step = local // halves
    block = (ranks, tiles, 2, step, TILE)
    base = first // tiles
    flops = 2 * 3 * (2 * energies) ** 2 * slots * TILE
    return pl.pallas_call(
        functools.partial(correlate_body, tiles, halves, float(energies) ** -1.5),
        grid=(slots // tiles,),
        out_shape=[jax.ShapeDtypeStruct((ranks, per_rank, 2, step, TILE), BF16)] * halves,
        in_specs=[
            pl.BlockSpec(table.shape, lambda g: (0, 0)),
            pl.BlockSpec((ranks, tiles, 2, 2, local, TILE), lambda g: (0, g, 0, 0, 0, 0)),
        ]
        + [pl.BlockSpec(memory_space=pl.ANY)] * len(previous),
        out_specs=[pl.BlockSpec(block, lambda g: (0, base + g, 0, 0, 0))] * halves,
        input_output_aliases={2 + h: h for h in range(len(previous))},
        compiler_params=pltpu.CompilerParams(vmem_limit_bytes=48 << 20),
        cost_estimate=pl.CostEstimate(flops=flops, bytes_accessed=12 << 20, transcendentals=0),
        name="correlate",
    )(table, data, *previous)


def sandwich_body(count, own, below, above, even, left_w, own_w, right_w, outer, *rest):
    diag_out, lower_out = rest[-2:]

    def spread(tiles, which):
        mask = even[which]
        zero = jnp.zeros((), BF16)
        halves = [jnp.where(mask > 0.5, tiles, zero), jnp.where(mask > 0.5, zero, tiles)]
        return jnp.concatenate(halves, axis=1)

    def times(tiles, which, matrix):
        stacked = jnp.concatenate([spread(tiles[0, k], which) for k in range(count)], axis=0)
        return jnp.dot(stacked, matrix[...], preferred_element_type=F32).astype(BF16)

    low, mid, top = times(below, 0, left_w), times(own, 1, own_w), times(above, 2, right_w)
    for k in range(count):
        here = slice(k * NNZ, (k + 1) * NNZ)
        inner = jnp.concatenate([low[here], mid[here]], axis=0)
        both = jnp.dot(outer[:, : 2 * NNZ], inner, preferred_element_type=F32)
        last = jnp.dot(outer[:, 2 * NNZ:], top[here], preferred_element_type=F32)
        width = last.shape[1]
        diag_out[0, k, 0] = (both[:, :width] + last).astype(BF16)
        lower_out[0, k, 0] = both[:, width:].astype(BF16)


def sandwich(own, below, above, even, weights, local, half, previous):
    left_w, own_w, right_w, outer = weights
    step, width = own.shape[1], outer.shape[0]
    count = min(4, step)
    base = half * step // count
    moving = pl.BlockSpec((1, count, NNZ, TILE), lambda p, g: (p, g, 0, 0))
    fixed = [pl.BlockSpec(w.shape, lambda p, g, n=w.ndim: (0,) * n) for w in (even,) + weights]
    out = jax.ShapeDtypeStruct((2, local, 1, width, width), BF16)
    out_spec = pl.BlockSpec((1, count, 1, width, width), lambda p, g: (p, base + g, 0, 0, 0))
    return pl.pallas_call(
        functools.partial(sandwich_body, count),
        grid=(2, step // count),
        out_shape=[out, out],
        in_specs=[moving] * 3 + fixed + [pl.BlockSpec(memory_space=pl.ANY)] * len(previous),
        out_specs=[out_spec, out_spec],
        input_output_aliases={8 + h: h for h in range(len(previous))},
        compiler_params=pltpu.CompilerParams(vmem_limit_bytes=48 << 20),
        cost_estimate=pl.CostEstimate(
            flops=2 * step * 2 * 1280 * 256 * 256,
            bytes_accessed=2 * step * (2 * width * width + 3 * NNZ * TILE) * 2,
            transcendentals=0,
        ),
        name="sandwich",
    )(own, below, above, even, left_w, own_w, right_w, outer, *previous)


def per_device(lesser, greater, vdiag, vlower, occupancy, tile_order):
    ranks = lax.axis_size("energy")
    local = lesser.shape[1]
    width = vdiag.shape[1]
    per_rank = NNZ // ranks
    late = max(1, per_rank // 4)
    chunks = [(0, per_rank - late), (per_rank - late, late)]
    halves = 2 if local >= 32 else 1
    counts, order = occupancy[0], tile_order[0]
    lesser = lesser.reshape(2, local, -1)
    greater = greater.reshape(2, local, -1)
    table = fourier_table(ranks * local)

    received = []
    for first, slots in chunks:
        packed, listing = pack(counts, order, lesser, greater, ranks, per_rank, first, slots)
        received.append(lax.all_to_all(packed, "energy", split_axis=0, concat_axis=0, tiled=True))

    diag_here, lower_here = vdiag[0], vlower[0]
    below_diag, below_list = passed_along((diag_here, listing), "space", 1)
    above_lower, above_list = passed_along((lower_here, listing), "space", -1)
    lists = jnp.stack([below_list, listing, above_list])
    even = (lists % 2 == 0).astype(F32)[:, :, None]
    rows = jnp.arange(width, dtype=jnp.int32)
    scatter = (rows[None, :, None] == (lists // 2)[:, None, :]).astype(BF16)
    outer = jnp.concatenate(
        [
            jnp.dot(lower_here, scatter[0], preferred_element_type=F32).astype(BF16),
            jnp.dot(diag_here, scatter[1], preferred_element_type=F32).astype(BF16),
            jnp.dot(above_lower.T, scatter[2], preferred_element_type=F32).astype(BF16),
        ],
        axis=1,
    )
    weights = (
        jnp.concatenate([lower_here.T, below_diag], axis=1),
        jnp.concatenate([diag_here, lower_here.T], axis=1),
        above_lower,
        outer,
    )

    polar = []
    for (first, _), data in zip(chunks, received):
        polar = correlate(table, data, per_rank, first, halves, polar)
    outs = []
    for h in range(halves):
        back = lax.all_to_all(polar[h], "energy", split_axis=0, concat_axis=0, tiled=True)
        own = back.reshape(NNZ, 2, local // halves, TILE).transpose(1, 2, 0, 3)
        below = passed_along(own, "space", 1)
        above = passed_along(own, "space", -1)
        outs = sandwich(own, below, above, even, weights, local, h, outs)
    return tuple(outs)


def solution(mesh):
    return jax.shard_map(
        per_device,
        mesh=mesh,
        in_specs=(
            P(None, "energy", "space", None),
            P(None, "energy", "space", None),
            P("space", None, None),
            P("space", None, None),
            P("space", None),
            P("space", None),
        ),
        out_specs=(P(None, "energy", "space", None, None), P(None, "energy", "space", None, None)),
        check_vma=False,
    )
```

```python
import functools

import jax
import jax.numpy as jnp
import numpy as np
from jax import lax
from jax.experimental import pallas as pl
from jax.experimental.pallas import tpu as pltpu
from jax.sharding import PartitionSpec as P

TILE = 128
NNZ = 128
BF16 = jnp.bfloat16
F32 = jnp.float32


def passed_along(value, axis, steps):
    count = lax.axis_size(axis)
    leading, last = (max(0, -steps), min(count, count - steps))
    return lax.ppermute(value, axis, [(source, source + steps) for source in range(leading, last)])


def fourier_table(energies):
    grid = np.arange(energies)
    phase = 2.0 * np.pi * ((grid[:, None] * grid[None, :]) % energies) / energies
    cos, sin = np.cos(phase), np.sin(phase)
    return jnp.asarray(np.block([[cos, sin], [-sin, cos]]), BF16)


def pack_body(ranks, most, per_rank, first, slots, counts, order, lesser, greater, packed, listing, stage, sem, out_sem):
    def rank_step(r, j):
        def slot_step(s, j):
            tile = order[r * most + s]
            listing[j] = tile
            slot = j % per_rank - first

            @pl.when((slot >= 0) & (slot < slots))
            def _():
                columns = pl.ds(pl.multiple_of(tile * TILE, TILE), TILE)
                for which, source in enumerate((lesser, greater)):
                    pltpu.make_async_copy(
                        source.at[:, :, columns], stage.at[j // per_rank, slot, which], sem
                    ).start()

            return j + 1

        return lax.fori_loop(0, counts[r], slot_step, j)

    lax.fori_loop(0, ranks, rank_step, 0)
    pltpu.make_async_copy(stage, stage, sem).wait()
    written = pltpu.make_async_copy(stage, packed, out_sem)
    written.start()
    written.wait()


def pack(counts, order, lesser, greater, ranks, per_rank, first, slots):
    local = lesser.shape[1]
    anywhere = pl.BlockSpec(memory_space=pl.ANY)
    scalars = pl.BlockSpec(memory_space=pltpu.SMEM)
    moved = 2 * ranks * slots * 4 * local * TILE * 2
    return pl.pallas_call(
        functools.partial(pack_body, ranks, 2 * NNZ // ranks, per_rank, first, slots),
        out_shape=(
            jax.ShapeDtypeStruct((ranks, slots, 2, 2, local, TILE), BF16),
            jax.ShapeDtypeStruct((NNZ,), jnp.int32),
        ),
        in_specs=[scalars, scalars, anywhere, anywhere],
        out_specs=(anywhere, scalars),
        scratch_shapes=[
            pltpu.VMEM((ranks, slots, 2, 2, local, TILE), BF16),
            pltpu.SemaphoreType.DMA,
            pltpu.SemaphoreType.DMA,
        ],
        compiler_params=pltpu.CompilerParams(vmem_limit_bytes=60 << 20),
        cost_estimate=pl.CostEstimate(flops=0, bytes_accessed=moved, transcendentals=0),
        name="pack",
    )(counts, order, lesser, greater)


def correlate_body(tiles, halves, factor, table, data, *rest):
    outs = rest[-halves:]
    ranks, _, _, _, local, _ = data.shape
    energies = ranks * local

    def part(tile, which, p):
        value = data[:, tile, which, p]
        if local % 16:
            return value.astype(F32).reshape(energies, TILE).astype(BF16)
        return value.reshape(energies, TILE)

    def columns(which, order):
        return jnp.concatenate(
            [jnp.concatenate([part(t, which, p) for p in order], axis=0) for t in range(tiles)],
            axis=1,
        )

    first = jnp.dot(table[...], columns(0, (0, 1)), preferred_element_type=F32)
    second = jnp.dot(table[...], columns(1, (1, 0)), preferred_element_type=F32)
    first_re, first_im = first[:energies], first[energies:]
    second_im, second_re = second[:energies], second[energies:]
    product = jnp.concatenate(
        [
            (first_re * second_im + first_im * second_re).astype(BF16),
            (first_re * second_re - first_im * second_im).astype(BF16),
        ],
        axis=0,
    )
    polar = jnp.dot(table[...], product, preferred_element_type=F32) * factor
    step = local // halves
    for t in range(tiles):
        for p in range(2):
            value = polar[(1 - p) * energies:(2 - p) * energies, t * TILE:(t + 1) * TILE]
            value = value.reshape(ranks, local, TILE).astype(BF16)
            for h in range(halves):
                outs[h][:, t, p] = value[:, h * step:(h + 1) * step]


def correlate(table, data, per_rank, first, halves, previous):
    ranks, slots, _, _, local, _ = data.shape
    energies = ranks * local
    tiles = 2 if slots % 2 == 0 else 1
    step = local // halves
    block = (ranks, tiles, 2, step, TILE)
    base = first // tiles
    flops = 2 * 3 * (2 * energies) ** 2 * slots * TILE
    return pl.pallas_call(
        functools.partial(correlate_body, tiles, halves, float(energies) ** -1.5),
        grid=(slots // tiles,),
        out_shape=[jax.ShapeDtypeStruct((ranks, per_rank, 2, step, TILE), BF16)] * halves,
        in_specs=[
            pl.BlockSpec(table.shape, lambda g: (0, 0)),
            pl.BlockSpec((ranks, tiles, 2, 2, local, TILE), lambda g: (0, g, 0, 0, 0, 0)),
        ]
        + [pl.BlockSpec(memory_space=pl.ANY)] * len(previous),
        out_specs=[pl.BlockSpec(block, lambda g: (0, base + g, 0, 0, 0))] * halves,
        input_output_aliases={2 + h: h for h in range(len(previous))},
        compiler_params=pltpu.CompilerParams(vmem_limit_bytes=48 << 20),
        cost_estimate=pl.CostEstimate(flops=flops, bytes_accessed=12 << 20, transcendentals=0),
        name="correlate",
    )(table, data, *previous)


def sandwich_body(count, own, below, above, even, left_w, own_w, right_w, outer, *rest):
    diag_out, lower_out = rest[-2:]

    def spread(tiles, which):
        mask = even[which]
        zero = jnp.zeros((), BF16)
        halves = [jnp.where(mask > 0.5, tiles, zero), jnp.where(mask > 0.5, zero, tiles)]
        return jnp.concatenate(halves, axis=1)

    def times(tiles, which, matrix):
        stacked = jnp.concatenate([spread(tiles[0, k], which) for k in range(count)], axis=0)
        return jnp.dot(stacked, matrix[...], preferred_element_type=F32).astype(BF16)

    low, mid, top = times(below, 0, left_w), times(own, 1, own_w), times(above, 2, right_w)
    for k in range(count):
        here = slice(k * NNZ, (k + 1) * NNZ)
        inner = jnp.concatenate([low[here], mid[here]], axis=0)
        both = jnp.dot(outer[:, : 2 * NNZ], inner, preferred_element_type=F32)
        last = jnp.dot(outer[:, 2 * NNZ:], top[here], preferred_element_type=F32)
        width = last.shape[1]
        diag_out[0, k, 0] = (both[:, :width] + last).astype(BF16)
        lower_out[0, k, 0] = both[:, width:].astype(BF16)


def sandwich(own, below, above, even, weights, local, half, previous):
    left_w, own_w, right_w, outer = weights
    step, width = own.shape[1], outer.shape[0]
    count = min(4, step)
    base = half * step // count
    moving = pl.BlockSpec((1, count, NNZ, TILE), lambda p, g: (p, g, 0, 0))
    fixed = [pl.BlockSpec(w.shape, lambda p, g, n=w.ndim: (0,) * n) for w in (even,) + weights]
    out = jax.ShapeDtypeStruct((2, local, 1, width, width), BF16)
    out_spec = pl.BlockSpec((1, count, 1, width, width), lambda p, g: (p, base + g, 0, 0, 0))
    return pl.pallas_call(
        functools.partial(sandwich_body, count),
        grid=(2, step // count),
        out_shape=[out, out],
        in_specs=[moving] * 3 + fixed + [pl.BlockSpec(memory_space=pl.ANY)] * len(previous),
        out_specs=[out_spec, out_spec],
        input_output_aliases={8 + h: h for h in range(len(previous))},
        compiler_params=pltpu.CompilerParams(vmem_limit_bytes=48 << 20),
        cost_estimate=pl.CostEstimate(
            flops=2 * step * 2 * 1280 * 256 * 256,
            bytes_accessed=2 * step * (2 * width * width + 3 * NNZ * TILE) * 2,
            transcendentals=0,
        ),
        name="sandwich",
    )(own, below, above, even, left_w, own_w, right_w, outer, *previous)


def per_device(lesser, greater, vdiag, vlower, occupancy, tile_order):
    ranks = lax.axis_size("energy")
    local = lesser.shape[1]
    width = vdiag.shape[1]
    per_rank = NNZ // ranks
    late = max(1, per_rank // 8)
    chunks = [(0, per_rank - late), (per_rank - late, late)]
    halves = 2 if local >= 32 else 1
    counts, order = occupancy[0], tile_order[0]
    lesser = lesser.reshape(2, local, -1)
    greater = greater.reshape(2, local, -1)
    table = fourier_table(ranks * local)

    def exchanged(value):
        return lax.all_to_all(value, "energy", split_axis=0, concat_axis=0, tiled=True)

    packs = []
    for first, slots in chunks:
        packed, listing = pack(counts, order, lesser, greater, ranks, per_rank, first, slots)
        packs.append(packed)
    early = exchanged(packs[0])

    diag_here, lower_here = vdiag[0], vlower[0]
    below_diag, below_list = passed_along((diag_here, listing), "space", 1)
    above_lower, above_list = passed_along((lower_here, listing), "space", -1)
    lists = jnp.stack([below_list, listing, above_list])
    even = (lists % 2 == 0).astype(F32)[:, :, None]
    rows = jnp.arange(width, dtype=jnp.int32)
    scatter = (rows[None, :, None] == (lists // 2)[:, None, :]).astype(BF16)
    outer = jnp.concatenate(
        [
            jnp.dot(lower_here, scatter[0], preferred_element_type=F32).astype(BF16),
            jnp.dot(diag_here, scatter[1], preferred_element_type=F32).astype(BF16),
            jnp.dot(above_lower.T, scatter[2], preferred_element_type=F32).astype(BF16),
        ],
        axis=1,
    )
    weights = (
        jnp.concatenate([lower_here.T, below_diag], axis=1),
        jnp.concatenate([diag_here, lower_here.T], axis=1),
        above_lower,
        outer,
    )

    held = lax.optimization_barrier((packs[1], early, weights, even))
    received = [held[1], exchanged(held[0])]
    weights, even = held[2], held[3]
    polar = []
    for (first, _), data in zip(chunks, received):
        polar = correlate(table, data, per_rank, first, halves, polar)
    outs = []
    for h in range(halves):
        back = exchanged(polar[h])
        own = back.reshape(NNZ, 2, local // halves, TILE).transpose(1, 2, 0, 3)
        below = passed_along(own, "space", 1)
        above = passed_along(own, "space", -1)
        outs = sandwich(own, below, above, even, weights, local, h, outs)
    return tuple(outs)


def solution(mesh):
    return jax.shard_map(
        per_device,
        mesh=mesh,
        in_specs=(
            P(None, "energy", "space", None),
            P(None, "energy", "space", None),
            P("space", None, None),
            P("space", None, None),
            P("space", None),
            P("space", None),
        ),
        out_specs=(P(None, "energy", "space", None, None), P(None, "energy", "space", None, None)),
        check_vma=False,
    )
```
